32 devices in a mesh: member: 4 (over z), space: 8 (over y, x, core).
Axes of the slice: x: 2, y: 2, z: 4, core: 2. Of those that a mesh axis runs over, the one named last changes fastest.
Arguments:
- tracers: float32 [8, 48, 8, 64, 128], P('member', None, None, 'space'), may hold values from -6 to 6
- horiz_mix: float32 [8, 64, 128], P(None, 'space'), may hold values from 0.05 to 0.22
- vert_mix: float32 [7, 64, 128], P(None, 'space'), may hold values from 0.02 to 0.2
- sunlit: int32 [64], replicated, may hold values from 0 to 1, as said below
- interaction: float32 [48, 48], replicated, may hold values from -0.875 to 0.875
- remin: float32 [48], replicated, may hold values from 0.05 to 0.3
- obs_cell: int32 [512], replicated, may hold values from 0 to 8191, as said below
- obs_tile: int32 [512], replicated, may hold values from 0 to 7
- obs_value: float32 [512], replicated, may hold values from -6 to 6
- obs_noise: float32 [8, 512], replicated, may hold values from -5 to 5
- obs_var: float32 [512], replicated, may hold values from 0.25 to 1
Outputs:
- analysis: float32 [8, 48, 8, 64, 128], P('member', None, None, 'space')
The draws below stay inside these ranges and needn't reach their ends.
Inputs may be any that keep to these rules, and one draw needn't show every extreme that they name: The sunlit rows are exactly those of half of the tiles, cyclically consecutive; each tile is wholly sunlit or wholly dark. `obs_cell`: an observation may lie in any tile; every tile uses at least one observation that lies in the tile 8 / 2 tiles on, counted round.
All inputs are finite; a program needn't handle non-finite values.
Results may differ from the reference program's by a relative error of at most 0.0003.
Values sent between devices are 32-bit elements; how exact they have to be, the bound alone decides.
No kernel may reach another device: no remote copies, remote signals or barrier semaphores. Data moves between devices by JAX's collectives and lax.ppermute only.
A program may use at most 64 MiB of HBM per device.

```python
import math
import jax
import jax.numpy as jnp
from jax import lax

NTR = 48
L = 8
COLS = 128
R = 8
NSUB = 4
MEMBERS = 8
ROWS = 64
NOBS = 512
N_SPACE = 8


def draw_sunlit(key, part):
    first_tile = jax.random.randint(key, (), 0, N_SPACE)
    tile_of_row = jnp.arange(ROWS, dtype=jnp.int32) // R
    return ((tile_of_row - first_tile) % N_SPACE < N_SPACE // 2).astype(jnp.int32)


def observation_layout(key):
    base_key = jax.random.fold_in(key, 11)
    key_tile, key_offset, key_place = jax.random.split(base_key, 3)
    obs_ids = jnp.arange(NOBS, dtype=jnp.int32)
    leading = obs_ids < N_SPACE
    tile_number = jnp.where(leading, obs_ids % N_SPACE, jax.random.randint(key_tile, (NOBS,), 0, N_SPACE))
    offset = jnp.where(leading, N_SPACE // 2, jax.random.randint(key_offset, (NOBS,), 0, N_SPACE))
    home_tile = (tile_number + offset) % N_SPACE
    place = jax.random.randint(key_place, (NOBS,), 0, R * COLS)
    return (tile_number.astype(jnp.int32), (home_tile * (R * COLS) + place).astype(jnp.int32))


def draw_obs_cell(key, part):
    return observation_layout(key)[1]


def draw_obs_tile(key, part):
    return observation_layout(key)[0]


def levels(rng, extent, cuts, low, high):
    def one(dim, shards_of):
        heights = jax.random.uniform(jax.random.fold_in(jax.random.fold_in(rng, 6), dim), (shards_of,), jnp.float32, low / len(cuts), high / len(cuts))
        return jnp.repeat(jnp.exp(heights), extent[dim] // shards_of).reshape((-1,) + (1,) * (len(extent) - dim - 1))

    loudness = one(*cuts[0])
    for cut in cuts[1:]:
        loudness = loudness * one(*cut)
    return loudness


def normal_values(key, shape, width, limit, pieces=(), held_as=jnp.bfloat16):
    drawn = jax.random.normal(key, shape, jnp.float32) * width
    if len(pieces) > 0:
        drawn = levels(key, shape, pieces, -0.22, 0.18) * drawn
    return jnp.clip(drawn, min=-limit, max=limit).astype(held_as)


def setup_inputs(seed: int = 0) -> dict:
    keys = jax.random.split(jax.random.key(seed), 12)
    return {
        "tracers": normal_values(keys[0], (MEMBERS, NTR, L, ROWS, COLS), 1.0, 6.0, ((0, 4), (3, 8)), jnp.float32),
        "horiz_mix": jnp.clip(0.05 + 0.17 * jax.random.uniform(keys[1], (L, ROWS, COLS), jnp.float32) ** levels(keys[1], (L, ROWS, COLS), ((1, 8),), -0.2, 0.2), 0.05, 0.22),
        "vert_mix": jnp.clip(0.02 + 0.18 * jax.random.uniform(keys[2], (L - 1, ROWS, COLS), jnp.float32) ** levels(keys[2], (L - 1, ROWS, COLS), ((1, 8),), -0.2, 0.2), 0.02, 0.2),
        "sunlit": draw_sunlit(jax.random.fold_in(keys[11], 71), 0),
        "interaction": normal_values(keys[4], (NTR, NTR), NTR ** -0.5, 0.875, (), jnp.float32),
        "remin": jnp.clip(jnp.exp(jax.random.uniform(keys[5], (NTR,), jnp.float32, math.log(0.05), math.log(0.3))), 0.05, 0.3),
        "obs_cell": draw_obs_cell(jax.random.fold_in(keys[11], 71), 0),
        "obs_tile": draw_obs_tile(jax.random.fold_in(keys[11], 71), 0),
        "obs_value": normal_values(keys[8], (NOBS,), 1.0, 6.0, (), jnp.float32),
        "obs_noise": normal_values(keys[9], (MEMBERS, NOBS), 0.7, 5.0, (), jnp.float32),
        "obs_var": jnp.clip(jnp.exp(jax.random.uniform(keys[10], (NOBS,), jnp.float32, math.log(0.25), math.log(1.0))), 0.25, 1.0),
    }


def sunlit_update(column_block, interaction, remin, light_levels):
    fraction = 1.0 / NSUB
    light_shape = (1, 1, -1) + (1,) * (column_block.ndim - 3)
    remin_shape = (1, -1) + (1,) * (column_block.ndim - 2)
    for substep in range(NSUB):
        uptake = jnp.einsum('ji,mi...->mj...', interaction, column_block, precision=lax.Precision.HIGHEST)
        column_block = column_block + fraction * (light_levels.reshape(light_shape) * jnp.tanh(uptake) - remin.reshape(remin_shape) * column_block)
    return column_block

def dark_update(column_block, remin):
    fraction = 1.0 / NSUB
    remin_shape = (1, -1) + (1,) * (column_block.ndim - 2)
    for substep in range(NSUB):
        column_block = column_block - fraction * (remin.reshape(remin_shape) * column_block)
    return column_block

def vertical_mixing(state, vert_mix):
    vertical_flux = vert_mix[None, None] * (state[:, :, 1:] - state[:, :, :-1])
    zero_layer = jnp.zeros_like(state[:, :, :1])
    return state + jnp.concatenate([vertical_flux, zero_layer], axis=2) - jnp.concatenate([zero_layer, vertical_flux], axis=2)

def reference(tracers, horiz_mix, vert_mix, sunlit, interaction, remin, obs_cell, obs_tile, obs_value, obs_noise, obs_var):
    padded = jnp.pad(tracers, ((0, 0), (0, 0), (0, 0), (1, 1), (1, 1)), mode='edge')
    laplace = padded[..., :-2, 1:-1] + padded[..., 2:, 1:-1] + padded[..., 1:-1, :-2] + padded[..., 1:-1, 2:] - 4.0 * tracers
    state = tracers + horiz_mix[None, None] * laplace
    state = vertical_mixing(state, vert_mix)
    light_levels = 0.6 * jnp.exp(-0.4 * jnp.arange(L, dtype=jnp.float32))
    lit_state = sunlit_update(state, interaction, remin, light_levels)
    dark_state = dark_update(state, remin)
    state = jnp.where((sunlit > 0)[None, None, None, :, None], lit_state, dark_state)
    surface = state[:, 0, 0].reshape(MEMBERS, ROWS * COLS)
    observed = jnp.take(surface, obs_cell, axis=1)
    spread = observed - jnp.mean(observed, axis=0, keepdims=True)
    innov = obs_value[None, :] + obs_noise - observed

    def tile_weights(tile_number):
        selection = jnp.where(obs_tile == tile_number, 1.0 / obs_var, 0.0)
        scaled = spread * selection[None, :]
        gram_matrix = (MEMBERS - 1) * jnp.eye(MEMBERS, dtype=jnp.float32) + jnp.dot(scaled, spread.T, precision=lax.Precision.HIGHEST)
        right_side = jnp.dot(scaled, innov.T, precision=lax.Precision.HIGHEST)
        weights = jnp.linalg.solve(gram_matrix, right_side)
        return weights - jnp.mean(weights, axis=0, keepdims=True)
    all_weights = lax.map(tile_weights, jnp.arange(N_SPACE, dtype=jnp.int32))
    tiled = state.reshape(MEMBERS, NTR, L, N_SPACE, R, COLS)
    increment = jnp.einsum('kabtrc,tkm->mabtrc', tiled, all_weights, precision=lax.Precision.HIGHEST)
    return (tiled + increment).reshape(MEMBERS, NTR, L, ROWS, COLS)
```

```python
import functools
import math

import jax
import jax.numpy as jnp
from jax import lax
from jax.experimental import pallas as pl
from jax.experimental.pallas import tpu as pltpu
from jax.sharding import PartitionSpec as P

NSUB = 4
ANY = pl.BlockSpec(memory_space=pl.ANY)
VMEM = pl.BlockSpec(memory_space=pltpu.VMEM)
SMEM = pl.BlockSpec(memory_space=pltpu.SMEM)


def row_sets(rows, n):
    first = list(range(1, 1 + n))
    rest = [r for r in range(rows) if r not in first]
    return [first] + [rest[i : i + n] for i in range(0, len(rest), n)]


def pick(values, index):
    out = jnp.int32(values[0])
    for i, value in enumerate(values[1:], 1):
        out = jnp.where(index == i, jnp.int32(value), out)
    return out


def split(value):
    high = value.astype(jnp.bfloat16)
    low = (value - high.astype(jnp.float32)).astype(jnp.bfloat16)
    return high, low


def edges_kernel(tracers, top, bottom):
    pairs, ntr, levels, rows, cols = tracers.shape
    flat = tracers.reshape(pairs, ntr * levels * rows, cols)
    for l in range(levels):
        for m in range(pairs):
            top[l, m] = flat[m, pl.ds(l * rows, ntr, stride=levels * rows), :]
            bottom[l, m] = flat[m, pl.ds(l * rows + rows - 1, ntr, stride=levels * rows), :]


def state_kernel(rows_of, l0, l1, n, halo, sunlit, tracers, horiz, vert, inter, remin, *refs):
    pairs, ntr, levels, rows, cols = tracers.shape
    if halo:
        north_halo, south_halo = refs[:2]
        refs = refs[2:]
    pieces, refs = refs[:n], refs[n:]
    surface = None
    if l0 == 0:
        surface, refs = refs[0], refs[1:]
    raw4, state, in_sem, out_sem = refs
    lo, hi = max(l0 - 1, 0), min(l1 + 1, levels)
    nin, nl = hi - lo, l1 - l0
    me = lax.axis_index("member")
    tile = lax.axis_index("space")
    count = lax.axis_size("space")
    copies = [
        pltpu.make_async_copy(tracers.at[m, :, lo:hi], raw4.at[m], in_sem.at[m]) for m in range(pairs)
    ]
    for copy in copies:
        copy.start()
    raw = raw4.reshape(pairs, ntr * nin * rows, cols)
    lane = lax.broadcasted_iota(jnp.int32, (ntr, cols), 1)
    for copy in copies:
        copy.wait()

    def strip(m, l, r):
        return raw[m, pl.ds((l - lo) * rows + r, ntr, stride=nin * rows), :]

    def mix(s, carry):
        r = pick(rows_of, me ^ s)
        if halo:
            up, down = jnp.maximum(r - 1, 0), jnp.minimum(r + 1, rows - 1)
            far_up = jnp.logical_and(r == 0, tile > 0)
            far_down = jnp.logical_and(r == rows - 1, tile < count - 1)
        else:
            up, down = r - 1, r + 1
        for m in range(pairs):
            mixed = {}
            for l in range(lo, hi):
                here = strip(m, l, r)
                north, south = strip(m, l, up), strip(m, l, down)
                if halo:
                    north = jnp.where(far_up, north_halo[l, m], north)
                    south = jnp.where(far_down, south_halo[l, m], south)
                west = jnp.where(lane == 0, here, pltpu.roll(here, 1, 1))
                east = jnp.where(lane == cols - 1, here, pltpu.roll(here, cols - 1, 1))
                laplace = north + south + west + east - 4.0 * here
                mixed[l] = here + horiz[l, pl.ds(r, 1), :] * laplace
            flux = {
                l: vert[l, pl.ds(r, 1), :] * (mixed[l + 1] - mixed[l]) for l in range(lo, hi - 1)
            }
            for l in range(l0, l1):
                value = mixed[l]
                if l in flux:
                    value = value + flux[l]
                if l - 1 in flux:
                    value = value - flux[l - 1]
                state[s, l - l0, m] = value
        return carry

    lax.fori_loop(0, n, mix, 0)

    fraction = 1.0 / NSUB
    diagonal = lax.broadcasted_iota(jnp.int32, (ntr, ntr), 0) == lax.broadcasted_iota(
        jnp.int32, (ntr, ntr), 1
    )
    loss = jnp.sum(
        jnp.where(diagonal, jnp.broadcast_to(remin[...], (ntr, ntr)), 0.0), axis=1, keepdims=True
    )
    lit = sunlit[tile * rows] > 0
    width = math.gcd(nl, 2)
    groups = nl // width

    @pl.when(lit)
    def _():
        high, low = split(inter[...])
        matrix = jnp.concatenate([high, high, low], axis=1)
        loss_wide = jnp.broadcast_to(loss, (ntr, cols))

        def step(unit, carry):
            s, g = unit // groups, lax.rem(unit, groups)
            blocks = [(g * width + i, m) for i in range(width) for m in range(pairs)]
            values = [state[s, l, m] for l, m in blocks]
            light = [
                0.6 * jnp.exp(-0.4 * jnp.full((1, cols), (l + l0), jnp.int32).astype(jnp.float32))
                for l, m in blocks
            ]
            for _ in range(NSUB):
                whole = jnp.concatenate(values, axis=1)
                high, low = split(whole)
                uptake = jnp.dot(
                    matrix,
                    jnp.concatenate([high, low, high], axis=0),
                    preferred_element_type=jnp.float32,
                )
                grown = jnp.tanh(uptake)
                values = [
                    value + fraction * (light[i] * grown[:, i * cols : (i + 1) * cols] - loss_wide * value)
                    for i, value in enumerate(values)
                ]
            for (l, m), value in zip(blocks, values):
                state[s, l, m] = value
            return carry

        lax.fori_loop(0, n * groups, step, 0, unroll=2)

    @pl.when(jnp.logical_not(lit))
    def _():
        loss_wide = jnp.broadcast_to(loss, (ntr, cols))

        def step(s, carry):
            for l in range(nl):
                for m in range(pairs):
                    value = state[s, l, m]
                    for _ in range(NSUB):
                        value = value - fraction * (loss_wide * value)
                    state[s, l, m] = value
            return carry

        lax.fori_loop(0, n, step, 0)

    copies = [pltpu.make_async_copy(state.at[s], pieces[s], out_sem.at[s]) for s in range(n)]
    for copy in copies:
        copy.start()
    if surface is not None:
        for s in range(n):
            for m in range(pairs):
                surface[s, pl.ds(m, 1), :] = state[s, 0, m, 0:1, :]
    for copy in copies:
        copy.wait()


def pick_kernel(sets, n, rows, cell, *refs):
    surfaces, out = refs[:-1], refs[-1]
    pairs, cols = surfaces[0].shape[1:]
    me = lax.axis_index("member")
    tile = lax.axis_index("space")
    local = cell[...] - tile * (rows * cols)
    column = jnp.bitwise_and(local, cols - 1)
    nobs = local.shape[1]
    onehot = lax.broadcasted_iota(jnp.int32, (cols, nobs), 0) == column
    onehot = onehot.astype(jnp.float32).astype(jnp.bfloat16)
    values = jnp.concatenate([ref[s] for ref in surfaces for s in range(n)], axis=0)
    high, rest = values.astype(jnp.bfloat16), None
    rest = values - high.astype(jnp.float32)
    middle, low = split(rest)
    depth = values.shape[0]
    parts = jnp.dot(
        jnp.concatenate([high, middle, low], axis=0), onehot, preferred_element_type=jnp.float32
    )
    found = parts[:depth] + parts[depth : 2 * depth] + parts[2 * depth :]
    total = jnp.zeros((pairs, nobs), jnp.float32)
    place = 0
    for rows_of in sets:
        for s in range(n):
            first = pick(rows_of, me ^ s) * cols
            inside = jnp.logical_and(local >= first, local < first + cols)
            total = total + jnp.where(inside, found[place : place + pairs], 0.0)
            place += pairs
    out[...] = total


def weights_kernel(n, noise, value, var, tile_of, *refs):
    parts, out = refs[:-1], refs[-1]
    pairs = parts[0].shape[0]
    members = pairs * n
    me = lax.axis_index("member")
    tile = lax.axis_index("space")
    observed = jnp.concatenate([part[...] for part in parts], axis=0)
    noises = jnp.concatenate(
        [noise[pl.ds((me ^ s) * pairs + m, 1), :] for s in range(n) for m in range(pairs)], axis=0
    )
    spread = observed - jnp.sum(observed, axis=0, keepdims=True) * (1.0 / members)
    innov = value[...] + noises - observed
    selection = jnp.where(tile_of[...] == tile, 1.0 / var[...], 0.0)
    scaled = spread * selection
    both = lax.dot_general(
        scaled,
        jnp.concatenate([spread, innov], axis=0),
        (((1,), (1,)), ((), ())),
        precision=lax.Precision.HIGHEST,
        preferred_element_type=jnp.float32,
    )
    row = lax.broadcasted_iota(jnp.int32, (members, 2 * members), 0)
    col = lax.broadcasted_iota(jnp.int32, (members, 2 * members), 1)
    both = both + jnp.where(row == col, float(members - 1), 0.0)
    for p in range(members):
        pivot = both[p : p + 1, :] / both[p : p + 1, p : p + 1]
        both = jnp.where(row == p, pivot, both - both[:, p : p + 1] * pivot)
    weights = both[:, members:]
    centered = weights - jnp.sum(weights, axis=0, keepdims=True) * (1.0 / members)
    out[...] = centered + jnp.where(row == col, 1.0, 0.0)[:, :members]


def apply_kernel(n, nsets, matrix, *refs):
    inputs, outputs = refs[: n * nsets], refs[n * nsets :]
    pairs, ntr = inputs[0].shape[1:3]
    members = n * pairs
    for j in range(nsets):
        for t in range(0, ntr, 8):
            fields = [
                inputs[j * n + s][0, m, t : t + 8, :] for s in range(n) for m in range(pairs)
            ]
            for k in range(members):
                total = matrix[0, k] * fields[0]
                for i in range(1, members):
                    total = total + matrix[i, k] * fields[i]
                outputs[k // pairs][0, j, k % pairs, t : t + 8, :] = total


def place_kernel(sets, n, l0, l1, aliased, *refs):
    pieces = refs[:n]
    out, block4, sem = refs[n + aliased :]
    pairs, ntr, nl, rows, cols = block4.shape
    me = lax.axis_index("member")
    block = block4.reshape(pairs, ntr * nl * rows, cols)
    copies = []
    for m in range(pairs):
        for s in range(n):
            for j, rows_of in enumerate(sets):
                r = pick(rows_of, me ^ s)
                for l in range(nl):
                    block[m, pl.ds(l * rows + r, ntr, stride=nl * rows), :] = pieces[s][l, j, m]
        copies.append(pltpu.make_async_copy(block4.at[m], out.at[m, :, l0:l1], sem.at[m]))
        copies[-1].start()
    for copy in copies:
        copy.wait()


def on_device(
    tracers, horiz_mix, vert_mix, sunlit, interaction, remin, obs_cell, obs_tile, obs_value, obs_noise, obs_var
):
    pairs, ntr, levels, rows, cols = tracers.shape
    n = lax.axis_size("member")
    tiles = lax.axis_size("space")
    nobs = obs_cell.shape[0]
    assert n & (n - 1) == 0 and tiles & (tiles - 1) == 0 and rows % n == 0 and n <= rows - 2
    assert cols & (cols - 1) == 0 and ntr % 16 == 0
    sets = row_sets(rows, n)
    nsets = len(sets)
    f32 = jnp.float32

    def swap(value, axis, distance):
        size = lax.axis_size(axis)
        return lax.ppermute(value, axis, [(i, i ^ distance) for i in range(size)])

    def states(j, l0, l1, halos):
        nin = min(l1 + 1, levels) - max(l0 - 1, 0)
        halo = j > 0
        shapes = [jax.ShapeDtypeStruct((l1 - l0, pairs, ntr, cols), f32)] * n
        specs = [ANY] * n
        if l0 == 0:
            shapes.append(jax.ShapeDtypeStruct((n, pairs, cols), f32))
            specs.append(VMEM)
        return pl.pallas_call(
            functools.partial(state_kernel, sets[j], l0, l1, n, halo),
            out_shape=shapes,
            in_specs=[SMEM, ANY] + [VMEM] * (4 + 2 * halo),
            out_specs=specs,
            scratch_shapes=[
                pltpu.VMEM((pairs, ntr, nin, rows, cols), f32),
                pltpu.VMEM((n, l1 - l0, pairs, ntr, cols), f32),
                pltpu.SemaphoreType.DMA((pairs,)),
                pltpu.SemaphoreType.DMA((n,)),
            ],
            name=f"state_{j}_{l0}_{l1}",
        )(sunlit, tracers, horiz_mix, vert_mix, interaction, remin.reshape(1, ntr), *(halos if halo else ()))

    half = levels // 2
    quarter = max(levels // 4, 1)
    cuts = {0: [0, quarter, levels]}
    for j in range(1, nsets):
        cuts[j] = [0, half, levels]
    groups = [(l, min(l + quarter, levels)) for l in range(0, levels, quarter)]

    chunks = {}
    surfaces = {}

    def run_chunk(j, l0, l1, halos=None):
        out = states(j, l0, l1, halos)
        if l0 == 0:
            surfaces[j] = out[n]
        chunks[j, l0, l1] = [out[0]] + [swap(out[s], "member", s) for s in range(1, n)]

    run_chunk(0, cuts[0][0], cuts[0][1])
    top, bottom = pl.pallas_call(
        edges_kernel,
        out_shape=[jax.ShapeDtypeStruct((levels, pairs, ntr, cols), f32)] * 2,
        in_specs=[VMEM],
        out_specs=[VMEM] * 2,
        name="edges",
    )(tracers)
    north = lax.ppermute(bottom, "space", [(i, i + 1) for i in range(tiles - 1)])
    south = lax.ppermute(top, "space", [(i + 1, i) for i in range(tiles - 1)])
    for a, b in zip(cuts[0][1:], cuts[0][2:]):
        run_chunk(0, a, b)
    for j in range(1, nsets):
        for a, b in zip(cuts[j], cuts[j][1:]):
            run_chunk(j, a, b, (north, south))

    own = pl.pallas_call(
        functools.partial(pick_kernel, sets, n, rows),
        out_shape=jax.ShapeDtypeStruct((pairs, nobs), f32),
        in_specs=[VMEM] * (1 + nsets),
        out_specs=VMEM,
        name="pick",
    )(obs_cell.reshape(1, nobs), *[surfaces[j] for j in range(nsets)])
    distance = 1
    while distance < tiles:
        own = own + swap(own, "space", distance)
        distance *= 2
    parts = [own] + [swap(own, "member", s) for s in range(1, n)]
    matrix = pl.pallas_call(
        functools.partial(weights_kernel, n),
        out_shape=jax.ShapeDtypeStruct((pairs * n, pairs * n), f32),
        in_specs=[VMEM] * (4 + n),
        out_specs=VMEM,
        name="weights",
    )(
        obs_noise,
        obs_value.reshape(1, nobs),
        obs_var.reshape(1, nobs),
        obs_tile.reshape(1, nobs),
        *parts,
    )

    def piece(j, l0):
        for (k, a, b), arrays in chunks.items():
            if k == j and a <= l0 < b:
                return arrays, a
        raise ValueError("no chunk")

    results = []
    for a, b in groups:
        inputs, specs = [], [SMEM]
        for j in range(nsets):
            arrays, base = piece(j, a)
            for array in arrays:
                inputs.append(array)
                specs.append(
                    pl.BlockSpec((1, pairs, ntr, cols), lambda g, o=a - base: (g + o, 0, 0, 0))
                )
        out = pl.pallas_call(
            functools.partial(apply_kernel, n, nsets),
            grid=(b - a,),
            out_shape=[jax.ShapeDtypeStruct((b - a, nsets, pairs, ntr, cols), f32)] * n,
            in_specs=specs,
            out_specs=[pl.BlockSpec((1, nsets, pairs, ntr, cols), lambda g: (g, 0, 0, 0, 0))] * n,
            name=f"apply_{a}",
        )(matrix, *inputs)
        results.append([out[0]] + [swap(out[s], "member", s) for s in range(1, n)])

    final = None
    for (a, b), arrays in zip(groups, results):
        aliased = final is not None
        final = pl.pallas_call(
            functools.partial(place_kernel, sets, n, a, b, aliased),
            out_shape=jax.ShapeDtypeStruct(tracers.shape, f32),
            in_specs=[VMEM] * n + [ANY] * aliased,
            out_specs=ANY,
            input_output_aliases={n: 0} if aliased else {},
            scratch_shapes=[
                pltpu.VMEM((pairs, ntr, b - a, rows, cols), f32),
                pltpu.SemaphoreType.DMA((pairs,)),
            ],
            name=f"place_{a}",
        )(*arrays, *([final] if aliased else []))
    return final


def solution(mesh):
    return jax.shard_map(
        on_device,
        mesh=mesh,
        in_specs=(
            P("member", None, None, "space", None),
            P(None, "space", None),
            P(None, "space", None),
        )
        + (P(),) * 8,
        out_specs=P("member", None, None, "space", None),
        check_vma=False,
    )
```
